32 devices in a mesh: row: 2 (over core), col: 4 (over y, x), mem: 4 (over z).
Axes of the slice: x: 2, y: 2, z: 4, core: 2. Of those that a mesh axis runs over, the one named last changes fastest.
Arguments:
- source_columns: bfloat16 [32768, 256], P(('mem', 'row', 'col')), parts along dimension 0, may hold values from -6 to 6
- tiles: bfloat16 [8, 4, 256, 128, 128], P(('mem', 'row'), 'col'), parts along dimension 0, may hold values from -0.15625 to 0.15625
- tile_index: int32 [8, 4, 256, 2], P(('mem', 'row'), 'col'), parts along dimension 0, may hold values from 0 to 31, as said below
- tile_count: int32 [8, 4], P(('mem', 'row'), 'col'), parts along dimension 0, may hold values from 32 to 256, as said below
Outputs:
- twice_coupled: bfloat16 [32768, 256], P(('mem', 'row', 'col')), parts along dimension 0
The draws below stay inside these ranges and needn't reach their ends.
There are 4 independent parts, one for each index of `mem`. The reference program is written for one: setup_inputs(seed, part) draws one part's arguments, and reference() takes and returns one part's arrays. A program takes and returns all parts, laid end to end along the dimension named above; each array names one. Nothing has to cross between parts.
Inputs may be any that keep to these rules, and one draw needn't show every extreme that they name: `tile_index`: slots k * 32 to (k + 1) * 32 - 1 of a device name every local block-row exactly once in their first entry; the panel block-columns of one block-row on one device all differ. Block-row entries lie in 0 to 31, block-column entries in 0 to 15. `tile_count`: each count is a multiple of 32; in every draw some device has all 256 slots live.
All inputs are finite; a program needn't handle non-finite values.
Results may differ from the reference program's by a relative error of at most 0.0049.
Values may be sent and summed in bfloat16 or wider, within the bound.
No kernel may reach another device: no remote copies, remote signals or barrier semaphores. Data moves between devices by JAX's collectives and lax.ppermute only.
A program may use at most 128 MiB of HBM per device.

```python
import jax
import jax.numpy as jnp
from jax import lax

TILE_SIZE = 128
BLOCK_ROWS = 32
LEVELS = 8
COLUMNS = 256
SLOT_COUNT = 256
SINGLETS = 8192
N_ROW = 2
N_COL = 4


def draw_tile_index(key, part):
    first_key, second_key = jax.random.split(jax.random.fold_in(key, 11))
    panel_total = BLOCK_ROWS * N_ROW // N_COL
    stride = panel_total // LEVELS
    scores = jax.random.randint(first_key, (N_ROW, N_COL, LEVELS, BLOCK_ROWS), 0, 1 << 20) * BLOCK_ROWS
    scores = scores + jnp.arange(BLOCK_ROWS, dtype=jnp.int32)
    row_part = jnp.argsort(scores, axis=-1, stable=True).astype(jnp.int32)
    offsets = jax.random.randint(second_key, (N_ROW, N_COL, LEVELS, BLOCK_ROWS), 0, stride)
    col_part = jnp.arange(LEVELS, dtype=jnp.int32)[:, None] * stride + offsets
    col_part = col_part.at[:, :, LEVELS - 1, 0].set(panel_total - 1)
    joined = jnp.stack([row_part, col_part.astype(jnp.int32)], axis=-1)
    return joined.reshape(N_ROW, N_COL, LEVELS * BLOCK_ROWS, 2).astype(jnp.int32)


def draw_tile_count(key, part):
    first_key, second_key = jax.random.split(jax.random.fold_in(key, 23))
    drawn = jax.random.randint(first_key, (N_ROW * N_COL,), 1, LEVELS // 2 + 1)
    fullest = jax.random.randint(second_key, (), 0, N_ROW * N_COL)
    levels_live = jnp.where(jnp.arange(N_ROW * N_COL, dtype=jnp.int32) == fullest, LEVELS, drawn)
    return (levels_live * BLOCK_ROWS).reshape(N_ROW, N_COL).astype(jnp.int32)


def level_of(rng, extent, shards, least, high):
    def one(position, blocks):
        draws = jax.random.uniform(jax.random.fold_in(jax.random.fold_in(rng, 6), position), (blocks,), jnp.float32, least / len(shards), high / len(shards))
        return jnp.repeat(jnp.exp(draws), extent[position] // blocks).reshape((-1,) + (1,) * (len(extent) - position - 1))

    gain = one(*shards[0])
    for cut in shards[1:]:
        gain = gain * one(*cut)
    return gain


def noise(key, extent, deviation, reach, pieces=(), kind=jnp.bfloat16):
    values = deviation * jax.random.normal(key, extent, jnp.float32)
    if pieces:
        values = values * level_of(key, extent, pieces, -0.22, 0.18)
    return jnp.clip(values, -reach, reach).astype(kind)


def setup_inputs(seed: int = 0, part: int = 0) -> dict:
    keys = jax.random.split(jax.random.key(seed), 5)
    own_keys = jax.random.split(jax.random.fold_in(keys[4], part), 5)
    return {
        "source_columns": noise(own_keys[0], (SINGLETS, COLUMNS), 1.0, 6.0, ((0, 8),)),
        "tiles": noise(own_keys[1], (N_ROW, N_COL, SLOT_COUNT, TILE_SIZE, TILE_SIZE), (TILE_SIZE * N_COL * 3) ** -0.5, 0.15625, ((0, 2), (1, 4))),
        "tile_index": draw_tile_index(jax.random.fold_in(jax.random.fold_in(keys[4], part), 71), part),
        "tile_count": draw_tile_count(jax.random.fold_in(jax.random.fold_in(keys[4], part), 71), part),
    }


def apply_once(values, tiles, tile_index, tile_count):
    grouped = values.reshape(N_ROW, N_COL, -1, COLUMNS)

    def one_row(row_at):
        def one_col(col_at):
            panel = lax.dynamic_index_in_dim(grouped, col_at, 1, keepdims=False)
            blocks_all = panel.reshape(-1, TILE_SIZE, COLUMNS)
            tile_set = tiles[row_at, col_at]
            index_set = tile_index[row_at, col_at]
            blocks = blocks_all[index_set[:, 1]]
            product = jnp.einsum("sij,sjn->sin", tile_set.astype(jnp.float32), blocks.astype(jnp.float32))
            live_mask = (jnp.arange(SLOT_COUNT, dtype=jnp.int32) < tile_count[row_at, col_at]).astype(jnp.float32)
            return jax.ops.segment_sum(product * live_mask[:, None, None], index_set[:, 0], num_segments=BLOCK_ROWS)

        return jnp.sum(lax.map(one_col, jnp.arange(N_COL, dtype=jnp.int32)), axis=0)

    summed = lax.map(one_row, jnp.arange(N_ROW, dtype=jnp.int32))
    return summed.reshape(-1, COLUMNS).astype(jnp.bfloat16)


def reference(source_columns, tiles, tile_index, tile_count):
    once = apply_once(source_columns, tiles, tile_index, tile_count)
    return apply_once(once, tiles, tile_index, tile_count)
```

```python
import functools

import jax
import jax.numpy as jnp
from jax import lax
from jax.experimental import pallas as pl
from jax.experimental.pallas import tpu as pltpu
from jax.sharding import PartitionSpec as P

TILE_SIZE = 128
BLOCK_ROWS = 32
COL_SHIFT = 16

QUARTERS = (3, 1, 2, 0)


def sweep_kernel(sources, outs_of_rows, *refs):
    table, tiles = refs[:2]
    source_refs = refs[2 : 2 + sources]
    out_refs = refs[2 + sources : -1]
    panel = refs[-1]
    at = 0
    for source in source_refs:
        panel[at : at + source.shape[0]] = source[...]
        at += source.shape[0]
    panel[at] = jnp.zeros_like(panel[at])
    levels = table.shape[1]
    first = 0
    for out, count in zip(out_refs, outs_of_rows):

        def row(b, carry, out=out, first=first):
            left, right = [], []
            for k in range(levels):
                entry = table[first + b, k]
                left.append(tiles[entry >> COL_SHIFT])
                right.append(panel[entry & ((1 << COL_SHIFT) - 1)])
            total = jnp.dot(
                jnp.concatenate(left, 1), jnp.concatenate(right, 0), preferred_element_type=jnp.float32
            )
            out[b] = total.astype(out.dtype)
            return carry

        lax.fori_loop(0, count, row, 0, unroll=4)
        first += count


def sweep(table, tiles, sources, outs):
    columns = sources[0].shape[-1]
    blocks = sum(s.shape[0] for s in sources)
    vmem = pl.BlockSpec(memory_space=pltpu.VMEM)
    return pl.pallas_call(
        functools.partial(sweep_kernel, len(sources), [n for n, _ in outs]),
        out_shape=[jax.ShapeDtypeStruct((n, TILE_SIZE, columns), dtype) for n, dtype in outs],
        in_specs=[pl.BlockSpec(memory_space=pltpu.SMEM)] + [vmem] * (1 + len(sources)),
        out_specs=[vmem] * len(outs),
        scratch_shapes=[pltpu.VMEM((blocks + 1, TILE_SIZE, columns), jnp.bfloat16)],
        compiler_params=pltpu.CompilerParams(vmem_limit_bytes=24 << 20),
    )(table, tiles, *sources)


def swap(values, mask, n_col):
    return lax.ppermute(values, "col", [(c, c ^ mask) for c in range(n_col)])


def row_table(tile_index, tile_count, n_row, n_col, blocks, own_first):
    index = tile_index.reshape(-1, BLOCK_ROWS, 2)
    levels = index.shape[0]
    rows, panel_block = index[..., 0], index[..., 1]
    if own_first:
        panel_block = panel_block ^ (lax.axis_index("row") * (BLOCK_ROWS // n_col))
    level = jnp.arange(levels, dtype=jnp.int32)[:, None]
    live = level * BLOCK_ROWS < tile_count.reshape(())
    slot = level * BLOCK_ROWS + jnp.arange(BLOCK_ROWS, dtype=jnp.int32)
    entry = (slot << COL_SHIFT) | jnp.where(live, panel_block, blocks)
    place = lax.axis_index("col")
    share = BLOCK_ROWS // n_col
    wanted = jnp.concatenate([(place ^ q) * share + jnp.arange(share, dtype=jnp.int32) for q in QUARTERS])
    hit = rows[None] == wanted[:, None, None]
    return jnp.sum(jnp.where(hit, entry[None], 0), axis=-1, dtype=jnp.int32)


def couple(values, table, tiles, n_row, n_col):
    share = BLOCK_ROWS // n_col
    half = share // 2
    f32, bf16 = jnp.float32, jnp.bfloat16
    blocks = values.reshape(share, TILE_SIZE, -1)
    if n_row == 2:
        sources = [blocks, lax.ppermute(blocks, "row", [(0, 1), (1, 0)])]
    else:
        sources = [lax.all_gather(blocks, "row", axis=0, tiled=True)]
    d_a, d_b = sweep(table[:share], tiles, sources, [(half, bf16), (half, bf16)])
    d_a, d_b = swap(d_a, 1, n_col), swap(d_b, 2, n_col)
    x_a, x_b, y_a, y_b = sweep(
        table[share : 3 * share], tiles, sources, [(half, bf16), (half, f32), (half, f32), (half, bf16)]
    )
    x_a, y_b = swap(x_a, 1, n_col), swap(y_b, 2, n_col)
    (own,) = sweep(table[3 * share :], tiles, sources, [(share, f32)])
    y_a = swap((y_a + d_a.astype(f32)).astype(bf16), 2, n_col)
    x_b = swap((x_b + d_b.astype(f32)).astype(bf16), 1, n_col)
    first = own[:half] + x_a.astype(f32) + y_a.astype(f32)
    second = own[half:] + y_b.astype(f32) + x_b.astype(f32)
    return jnp.concatenate([first, second], 0).astype(bf16).reshape(values.shape)


def local(n_row, n_col, source_columns, tiles, tile_index, tile_count):
    tiles = tiles.reshape(-1, TILE_SIZE, TILE_SIZE)
    blocks = n_row * BLOCK_ROWS // n_col
    table = row_table(tile_index, tile_count, n_row, n_col, blocks, n_row == 2)
    once = couple(source_columns, table, tiles, n_row, n_col)
    return couple(once, table, tiles, n_row, n_col)


def solution(mesh):
    n_row, n_col = mesh.shape["row"], mesh.shape["col"]
    assert n_col == 4
    placed = (
        P(("mem", "row", "col"), None),
        P(("mem", "row"), "col", None, None, None),
        P(("mem", "row"), "col", None, None),
        P(("mem", "row"), "col"),
    )
    return jax.shard_map(
        functools.partial(local, n_row, n_col),
        mesh=mesh,
        in_specs=placed,
        out_specs=P(("mem", "row", "col"), None),
        check_vma=False,
    )
```

```python
import functools

import jax
import jax.numpy as jnp
from jax import lax
from jax.experimental import pallas as pl
from jax.experimental.pallas import tpu as pltpu
from jax.sharding import PartitionSpec as P

TILE_SIZE = 128
BLOCK_ROWS = 32
COL_SHIFT = 16
CHUNK = 128
LOADS = 4

VMEM = pl.BlockSpec(memory_space=pltpu.VMEM)
SMEM = pl.BlockSpec(memory_space=pltpu.SMEM)
HBM = pl.BlockSpec(memory_space=pltpu.HBM)


def directions():
    core = lax.axis_index("row") % 2
    return 1 + core, 2 - core


def load_kernel(own_first, share, blocks, index, count, tiles, table, tiles_here, index_here, count_here, rows, sem):
    slots = tiles.shape[0]
    part = slots // LOADS
    small = [
        pltpu.make_async_copy(index, index_here.at[0:2], sem.at[LOADS]),
        pltpu.make_async_copy(count, count_here, sem.at[LOADS + 1]),
    ]
    copies = [
        pltpu.make_async_copy(
            tiles.at[pl.ds(i * part, part)], tiles_here.at[pl.ds(i * part, part)], sem.at[i]
        )
        for i in range(LOADS)
    ]
    for copy in small + copies:
        copy.start()
    lane = lax.broadcasted_iota(jnp.int32, (BLOCK_ROWS, TILE_SIZE), 1)
    quarter = lane // share
    first, second = directions()
    flip = jnp.where(quarter == 0, 3, jnp.where(quarter == 1, first, jnp.where(quarter == 2, second, 0)))
    wanted = (lax.axis_index("col") ^ flip) * share + lane % share
    slot = lax.broadcasted_iota(jnp.int32, (BLOCK_ROWS, 1), 0)
    for copy in small:
        copy.wait()
    by_slot = index_here[...].T
    for level in range(slots // BLOCK_ROWS):
        here = by_slot[level * BLOCK_ROWS : (level + 1) * BLOCK_ROWS]
        row, block = here[:, 0:1], here[:, 1:2]
        if own_first:
            block = block ^ (lax.axis_index("row") * share)
        block = jnp.where(level * BLOCK_ROWS < count_here[0, 0], block, blocks)
        entry = ((slot + level * BLOCK_ROWS) << COL_SHIFT) | block
        rows[level : level + 1] = jnp.sum(jnp.where(row == wanted, entry, 0), axis=0, keepdims=True)
    to_scalar = pltpu.make_async_copy(rows, table, sem.at[LOADS])
    to_scalar.start()
    to_scalar.wait()
    for copy in copies:
        copy.wait()


def load(tile_index, tile_count, tiles, own_first, share, blocks):
    slots = tiles.shape[0]
    levels = slots // BLOCK_ROWS
    return pl.pallas_call(
        functools.partial(load_kernel, own_first, share, blocks),
        out_shape=[pltpu.SMEM((levels, TILE_SIZE), jnp.int32), pltpu.VMEM(tiles.shape, tiles.dtype)],
        in_specs=[HBM, HBM, HBM],
        out_specs=[SMEM, VMEM],
        scratch_shapes=[
            pltpu.VMEM((8, slots), jnp.int32),
            pltpu.SMEM((1, 1), jnp.int32),
            pltpu.VMEM((levels, TILE_SIZE), jnp.int32),
            pltpu.SemaphoreType.DMA((LOADS + 2,)),
        ],
        compiler_params=pltpu.CompilerParams(vmem_limit_bytes=50 << 20),
    )(tile_index, tile_count, tiles)


def sweep_kernel(counts, first, sources, *refs):
    table, tiles = refs[:2]
    source_refs = refs[2 : 2 + sources]
    out_refs = refs[2 + sources : -1]
    panel = refs[-1]
    at = 0
    for source in source_refs:
        panel[at : at + source.shape[0]] = source[...]
        at += source.shape[0]
    panel[at] = jnp.zeros_like(panel[at])
    levels = table.shape[0]
    split = panel.shape[2] // CHUNK
    for i, count in enumerate(counts):
        outs = out_refs[i * split : (i + 1) * split]

        def row(b, carry, outs=outs, first=first):
            left, right = [], []
            for k in range(levels):
                entry = table[k, first + b]
                left.append(tiles[entry >> COL_SHIFT])
                right.append(panel[entry & ((1 << COL_SHIFT) - 1)])
            total = jnp.dot(
                jnp.concatenate(left, 1), jnp.concatenate(right, 0), preferred_element_type=jnp.float32
            )
            for j, out in enumerate(outs):
                out[b] = total[:, j * CHUNK : (j + 1) * CHUNK].astype(out.dtype)
            return carry

        lax.fori_loop(0, count, row, 0, unroll=4)
        first += count


def sweep(table, tiles, sources, first, outs):
    blocks = sum(s.shape[0] for s in sources)
    columns = sources[0].shape[2]
    split = columns // CHUNK
    rows, depth = sum(n for n, _ in outs), table.shape[0] * TILE_SIZE
    out = pl.pallas_call(
        functools.partial(sweep_kernel, [n for n, _ in outs], first, len(sources)),
        out_shape=[
            jax.ShapeDtypeStruct((n, TILE_SIZE, CHUNK), dtype) for n, dtype in outs for _ in range(split)
        ],
        in_specs=[SMEM] + [VMEM] * (1 + len(sources)),
        out_specs=[VMEM] * (len(outs) * split),
        scratch_shapes=[pltpu.VMEM((blocks + 1, TILE_SIZE, columns), jnp.bfloat16)],
        compiler_params=pltpu.CompilerParams(vmem_limit_bytes=12 << 20),
        cost_estimate=pl.CostEstimate(
            flops=2 * rows * TILE_SIZE * depth * columns * 2,
            transcendentals=0,
            bytes_accessed=rows * TILE_SIZE * (depth + columns) * 2,
        ),
    )(table, tiles, *sources)
    return [out[i * split : (i + 1) * split] for i in range(len(outs))]


def exchange(values, second, n_row, n_col):
    pairs = []
    for r in range(n_row):
        flip = 1 + r % 2
        if second:
            flip = 3 - flip
        pairs += [(r * n_col + c, r * n_col + (c ^ flip)) for c in range(n_col)]
    return lax.ppermute(values, ("row", "col"), pairs)


def panel_of(blocks, n_row):
    if n_row == 2:
        return [blocks, lax.ppermute(blocks, "row", [(0, 1), (1, 0)])]
    return [lax.all_gather(blocks, "row", axis=0, tiled=True)]


def local(n_row, n_col, source_columns, tiles, tile_index, tile_count):
    f32, bf16 = jnp.float32, jnp.bfloat16
    share = BLOCK_ROWS // n_col
    columns = source_columns.shape[1]
    split = columns // CHUNK
    blocks = n_row * share
    whole = panel_of(source_columns.reshape(share, TILE_SIZE, columns), n_row)
    table, tiles = load(
        tile_index.reshape(-1, 2).T, tile_count, tiles.reshape(-1, TILE_SIZE, TILE_SIZE), n_row == 2, share, blocks
    )

    first = functools.partial(exchange, second=False, n_row=n_row, n_col=n_col)
    second = functools.partial(exchange, second=True, n_row=n_row, n_col=n_col)

    def couple(source):
        (far,) = sweep(table, tiles, source, 0, [(share, bf16)])
        far = [first(f) for f in far]
        near, kept = sweep(table, tiles, source, share, [(share, bf16), (share, f32)])
        near = [first(n) for n in near]
        (own,) = sweep(table, tiles, source, 3 * share, [(share, f32)])
        last = [second((k + f.astype(f32)).astype(bf16)) for k, f in zip(kept, far)]
        return [(o + n.astype(f32) + t.astype(f32)).astype(bf16) for o, n, t in zip(own, near, last)]

    once = couple(whole)
    twice = [couple(panel_of(o, n_row))[0] for o in once]
    return jnp.concatenate(twice, -1).reshape(source_columns.shape)


def solution(mesh):
    n_row, n_col = mesh.shape["row"], mesh.shape["col"]
    assert n_col == 4
    placed = (
        P(("mem", "row", "col"), None),
        P(("mem", "row"), "col", None, None, None),
        P(("mem", "row"), "col", None, None),
        P(("mem", "row"), "col"),
    )
    return jax.shard_map(
        functools.partial(local, n_row, n_col),
        mesh=mesh,
        in_specs=placed,
        out_specs=P(("mem", "row", "col"), None),
        check_vma=False,
    )
```

```python
import functools

import jax
import jax.numpy as jnp
from jax import lax
from jax.experimental import pallas as pl
from jax.experimental.pallas import tpu as pltpu
from jax.sharding import PartitionSpec as P

TILE_SIZE = 128
BLOCK_ROWS = 32
COL_SHIFT = 16
CHUNK = 128
LOADS = 4

VMEM = pl.BlockSpec(memory_space=pltpu.VMEM)
SMEM = pl.BlockSpec(memory_space=pltpu.SMEM)
HBM = pl.BlockSpec(memory_space=pltpu.HBM)


def directions():
    core = lax.axis_index("row") % 2
    return 1 + core, 2 - core


def load_kernel(own_first, share, blocks, index, count, tiles, table, tiles_here, index_here, count_here, rows, sem):
    slots = tiles.shape[0]
    part = slots // LOADS
    small = [
        pltpu.make_async_copy(index, index_here.at[0:2], sem.at[LOADS]),
        pltpu.make_async_copy(count, count_here, sem.at[LOADS + 1]),
    ]
    copies = [
        pltpu.make_async_copy(
            tiles.at[pl.ds(i * part, part)], tiles_here.at[pl.ds(i * part, part)], sem.at[i]
        )
        for i in range(LOADS)
    ]
    for copy in small + copies:
        copy.start()
    lane = lax.broadcasted_iota(jnp.int32, (BLOCK_ROWS, TILE_SIZE), 1)
    quarter = lane // share
    first, second = directions()
    flip = jnp.where(quarter == 0, 3, jnp.where(quarter == 1, first, jnp.where(quarter == 2, second, 0)))
    wanted = (lax.axis_index("col") ^ flip) * share + lane % share
    slot = lax.broadcasted_iota(jnp.int32, (BLOCK_ROWS, 1), 0)
    for copy in small:
        copy.wait()
    by_slot = index_here[...].T
    for level in range(slots // BLOCK_ROWS):
        here = by_slot[level * BLOCK_ROWS : (level + 1) * BLOCK_ROWS]
        row, block = here[:, 0:1], here[:, 1:2]
        if own_first:
            block = block ^ (lax.axis_index("row") * share)
        block = jnp.where(level * BLOCK_ROWS < count_here[0, 0], block, blocks)
        entry = ((slot + level * BLOCK_ROWS) << COL_SHIFT) | block
        rows[level : level + 1] = jnp.sum(jnp.where(row == wanted, entry, 0), axis=0, keepdims=True)
    to_scalar = pltpu.make_async_copy(rows, table, sem.at[LOADS])
    to_scalar.start()
    to_scalar.wait()
    for copy in copies:
        copy.wait()


def load(tile_index, tile_count, tiles, own_first, share, blocks):
    slots = tiles.shape[0]
    levels = slots // BLOCK_ROWS
    return pl.pallas_call(
        functools.partial(load_kernel, own_first, share, blocks),
        out_shape=[pltpu.SMEM((levels, TILE_SIZE), jnp.int32), pltpu.VMEM(tiles.shape, tiles.dtype)],
        in_specs=[HBM, HBM, HBM],
        out_specs=[SMEM, VMEM],
        scratch_shapes=[
            pltpu.VMEM((8, slots), jnp.int32),
            pltpu.SMEM((1, 1), jnp.int32),
            pltpu.VMEM((levels, TILE_SIZE), jnp.int32),
            pltpu.SemaphoreType.DMA((LOADS + 2,)),
        ],
        compiler_params=pltpu.CompilerParams(vmem_limit_bytes=50 << 20),
    )(tile_index, tile_count, tiles)


def sweep_kernel(counts, first, sources, *refs):
    table, tiles = refs[:2]
    source_refs = refs[2 : 2 + sources]
    out_refs = refs[2 + sources : -1]
    panel = refs[-1]
    at = 0
    for source in source_refs:
        panel[at : at + source.shape[0]] = source[...]
        at += source.shape[0]
    panel[at] = jnp.zeros_like(panel[at])
    levels = table.shape[0]
    split = panel.shape[2] // CHUNK
    for i, count in enumerate(counts):
        outs = out_refs[i * split : (i + 1) * split]

        def row(b, carry, outs=outs, first=first):
            left, right = [], []
            for k in range(levels):
                entry = table[k, first + b]
                left.append(tiles[entry >> COL_SHIFT])
                right.append(panel[entry & ((1 << COL_SHIFT) - 1)])
            total = jnp.dot(
                jnp.concatenate(left, 1), jnp.concatenate(right, 0), preferred_element_type=jnp.float32
            )
            for j, out in enumerate(outs):
                out[b] = total[:, j * CHUNK : (j + 1) * CHUNK].astype(out.dtype)
            return carry

        lax.fori_loop(0, count, row, 0, unroll=8)
        first += count


def sweep(table, tiles, sources, first, outs):
    blocks = sum(s.shape[0] for s in sources)
    columns = sources[0].shape[2]
    split = columns // CHUNK
    out = pl.pallas_call(
        functools.partial(sweep_kernel, [n for n, _ in outs], first, len(sources)),
        out_shape=[
            jax.ShapeDtypeStruct((n, TILE_SIZE, CHUNK), dtype) for n, dtype in outs for _ in range(split)
        ],
        in_specs=[SMEM] + [VMEM] * (1 + len(sources)),
        out_specs=[VMEM] * (len(outs) * split),
        scratch_shapes=[pltpu.VMEM((blocks + 1, TILE_SIZE, columns), jnp.bfloat16)],
        compiler_params=pltpu.CompilerParams(vmem_limit_bytes=12 << 20),
    )(table, tiles, *sources)
    return [out[i * split : (i + 1) * split] for i in range(len(outs))]


def exchange(values, second, n_row, n_col):
    pairs = []
    for r in range(n_row):
        flip = 1 + r % 2
        if second:
            flip = 3 - flip
        pairs += [(r * n_col + c, r * n_col + (c ^ flip)) for c in range(n_col)]
    return lax.ppermute(values, ("row", "col"), pairs)


def panel_of(blocks, n_row):
    if n_row == 2:
        return [blocks, lax.ppermute(blocks, "row", [(0, 1), (1, 0)])]
    return [lax.all_gather(blocks, "row", axis=0, tiled=True)]


def local(n_row, n_col, source_columns, tiles, tile_index, tile_count):
    f32, bf16 = jnp.float32, jnp.bfloat16
    share = BLOCK_ROWS // n_col
    columns = source_columns.shape[1]
    split = columns // CHUNK
    blocks = n_row * share
    whole = panel_of(source_columns.reshape(share, TILE_SIZE, columns), n_row)
    table, tiles = load(
        tile_index.reshape(-1, 2).T, tile_count, tiles.reshape(-1, TILE_SIZE, TILE_SIZE), n_row == 2, share, blocks
    )

    first = functools.partial(exchange, second=False, n_row=n_row, n_col=n_col)
    second = functools.partial(exchange, second=True, n_row=n_row, n_col=n_col)

    def couple(source):
        (far,) = sweep(table, tiles, source, 0, [(share, bf16)])
        far = [first(f) for f in far]
        near, kept = sweep(table, tiles, source, share, [(share, bf16), (share, f32)])
        near = [first(n) for n in near]
        (own,) = sweep(table, tiles, source, 3 * share, [(share, f32)])
        last = [second((k + f.astype(f32)).astype(bf16)) for k, f in zip(kept, far)]
        return [(o + n.astype(f32) + t.astype(f32)).astype(bf16) for o, n, t in zip(own, near, last)]

    once = couple(whole)
    twice = [couple(panel_of(o, n_row))[0] for o in once]
    return jnp.concatenate(twice, -1).reshape(source_columns.shape)


def solution(mesh):
    n_row, n_col = mesh.shape["row"], mesh.shape["col"]
    assert n_col == 4
    placed = (
        P(("mem", "row", "col"), None),
        P(("mem", "row"), "col", None, None, None),
        P(("mem", "row"), "col", None, None),
        P(("mem", "row"), "col"),
    )
    return jax.shard_map(
        functools.partial(local, n_row, n_col),
        mesh=mesh,
        in_specs=placed,
        out_specs=P(("mem", "row", "col"), None),
        check_vma=False,
    )
```

```python
import functools

import jax
import jax.numpy as jnp
from jax import lax
from jax.experimental import pallas as pl
from jax.experimental.pallas import tpu as pltpu
from jax.sharding import PartitionSpec as P

TILE_SIZE = 128
BLOCK_ROWS = 32
COL_SHIFT = 16
CHUNK = 128
LOADS = 4

VMEM = pl.BlockSpec(memory_space=pltpu.VMEM)
SMEM = pl.BlockSpec(memory_space=pltpu.SMEM)
HBM = pl.BlockSpec(memory_space=pltpu.HBM)


def directions():
    core = lax.axis_index("row") % 2
    return 1 + core, 2 - core


def load_kernel(own_first, share, blocks, index, count, tiles, table, tiles_here, index_here, count_here, rows, sem):
    slots = tiles.shape[0]
    part = slots // LOADS
    small = [
        pltpu.make_async_copy(index, index_here.at[0:2], sem.at[LOADS]),
        pltpu.make_async_copy(count, count_here, sem.at[LOADS + 1]),
    ]
    copies = [
        pltpu.make_async_copy(
            tiles.at[pl.ds(i * part, part)], tiles_here.at[pl.ds(i * part, part)], sem.at[i]
        )
        for i in range(LOADS)
    ]
    for copy in small + copies:
        copy.start()
    lane = lax.broadcasted_iota(jnp.int32, (BLOCK_ROWS, TILE_SIZE), 1)
    quarter = lane // share
    first, second = directions()
    flip = jnp.where(quarter == 0, 3, jnp.where(quarter == 1, first, jnp.where(quarter == 2, second, 0)))
    wanted = (lax.axis_index("col") ^ flip) * share + lane % share
    slot = lax.broadcasted_iota(jnp.int32, (BLOCK_ROWS, 1), 0)
    for copy in small:
        copy.wait()
    by_slot = index_here[...].T
    for level in range(slots // BLOCK_ROWS):
        here = by_slot[level * BLOCK_ROWS : (level + 1) * BLOCK_ROWS]
        row, block = here[:, 0:1], here[:, 1:2]
        if own_first:
            block = block ^ (lax.axis_index("row") * share)
        block = jnp.where(level * BLOCK_ROWS < count_here[0, 0], block, blocks)
        entry = ((slot + level * BLOCK_ROWS) << COL_SHIFT) | block
        rows[level : level + 1] = jnp.sum(jnp.where(row == wanted, entry, 0), axis=0, keepdims=True)
    to_scalar = pltpu.make_async_copy(rows, table, sem.at[LOADS])
    to_scalar.start()
    to_scalar.wait()
    for copy in copies:
        copy.wait()


def load(tile_index, tile_count, tiles, own_first, share, blocks):
    slots = tiles.shape[0]
    levels = slots // BLOCK_ROWS
    return pl.pallas_call(
        functools.partial(load_kernel, own_first, share, blocks),
        out_shape=[pltpu.SMEM((levels, TILE_SIZE), jnp.int32), pltpu.VMEM(tiles.shape, tiles.dtype)],
        in_specs=[HBM, HBM, HBM],
        out_specs=[SMEM, VMEM],
        scratch_shapes=[
            pltpu.VMEM((8, slots), jnp.int32),
            pltpu.SMEM((1, 1), jnp.int32),
            pltpu.VMEM((levels, TILE_SIZE), jnp.int32),
            pltpu.SemaphoreType.DMA((LOADS + 2,)),
        ],
        compiler_params=pltpu.CompilerParams(vmem_limit_bytes=50 << 20),
    )(tile_index, tile_count, tiles)


def sweep_kernel(counts, first, sources, *refs):
    table, tiles = refs[:2]
    source_refs = refs[2 : 2 + sources]
    out_refs = refs[2 + sources : -1]
    panel = refs[-1]
    at = 0
    for source in source_refs:
        panel[at : at + source.shape[0]] = source[...]
        at += source.shape[0]
    panel[at] = jnp.zeros_like(panel[at])
    levels = table.shape[0]
    split = panel.shape[2] // CHUNK
    for i, count in enumerate(counts):
        outs = out_refs[i * split : (i + 1) * split]

        def row(b, carry, outs=outs, first=first):
            left, right = [], []
            for k in range(levels):
                entry = table[k, first + b]
                left.append(tiles[entry >> COL_SHIFT])
                right.append(panel[entry & ((1 << COL_SHIFT) - 1)])
            total = jnp.dot(
                jnp.concatenate(left, 1), jnp.concatenate(right, 0), preferred_element_type=jnp.float32
            )
            for j, out in enumerate(outs):
                out[b] = total[:, j * CHUNK : (j + 1) * CHUNK].astype(out.dtype)
            return carry

        lax.fori_loop(0, count, row, 0, unroll=8)
        first += count


def sweep(table, tiles, sources, first, outs):
    blocks = sum(s.shape[0] for s in sources)
    columns = sources[0].shape[2]
    split = columns // CHUNK
    out = pl.pallas_call(
        functools.partial(sweep_kernel, [n for n, _ in outs], first, len(sources)),
        out_shape=[
            jax.ShapeDtypeStruct((n, TILE_SIZE, CHUNK), dtype) for n, dtype in outs for _ in range(split)
        ],
        in_specs=[SMEM] + [VMEM] * (1 + len(sources)),
        out_specs=[VMEM] * (len(outs) * split),
        scratch_shapes=[pltpu.VMEM((blocks + 1, TILE_SIZE, columns), jnp.bfloat16)],
        compiler_params=pltpu.CompilerParams(vmem_limit_bytes=12 << 20),
    )(table, tiles, *sources)
    return [out[i * split : (i + 1) * split] for i in range(len(outs))]


def finish_kernel(column, own, near, last, *refs):
    out, here, sem = refs[-3:]
    count = own.shape[0]
    copies = []
    for b in range(count):
        total = own[b] + near[b].astype(jnp.float32) + last[b].astype(jnp.float32)
        rows = slice(b * TILE_SIZE, (b + 1) * TILE_SIZE)
        here[rows] = total.astype(here.dtype)
        copies.append(
            pltpu.make_async_copy(here.at[rows], out.at[rows, column : column + CHUNK], sem.at[b])
        )
        copies[-1].start()
    for copy in copies:
        copy.wait()


def finish(own, near, last, column, shape, earlier):
    return pl.pallas_call(
        functools.partial(finish_kernel, column),
        out_shape=pltpu.HBM(shape, jnp.bfloat16),
        in_specs=[VMEM] * 3 + [HBM] * len(earlier),
        out_specs=HBM,
        input_output_aliases={3: 0} if earlier else {},
        scratch_shapes=[
            pltpu.VMEM((shape[0], CHUNK), jnp.bfloat16),
            pltpu.SemaphoreType.DMA((own.shape[0],)),
        ],
        compiler_params=pltpu.CompilerParams(vmem_limit_bytes=8 << 20),
    )(own, near, last, *earlier)


def exchange(values, second, n_row, n_col):
    pairs = []
    for r in range(n_row):
        flip = 1 + r % 2
        if second:
            flip = 3 - flip
        pairs += [(r * n_col + c, r * n_col + (c ^ flip)) for c in range(n_col)]
    return lax.ppermute(values, ("row", "col"), pairs)


def panel_of(blocks, n_row):
    if n_row == 2:
        return [blocks, lax.ppermute(blocks, "row", [(0, 1), (1, 0)])]
    return [lax.all_gather(blocks, "row", axis=0, tiled=True)]


def local(n_row, n_col, source_columns, tiles, tile_index, tile_count):
    f32, bf16 = jnp.float32, jnp.bfloat16
    share = BLOCK_ROWS // n_col
    columns = source_columns.shape[1]
    split = columns // CHUNK
    blocks = n_row * share
    whole = panel_of(source_columns.reshape(share, TILE_SIZE, columns), n_row)
    table, tiles = load(
        tile_index.reshape(-1, 2).T, tile_count, tiles.reshape(-1, TILE_SIZE, TILE_SIZE), n_row == 2, share, blocks
    )

    first = functools.partial(exchange, second=False, n_row=n_row, n_col=n_col)
    second = functools.partial(exchange, second=True, n_row=n_row, n_col=n_col)

    def couple(source):
        (far,) = sweep(table, tiles, source, 0, [(share, bf16)])
        far = [first(f) for f in far]
        near, kept = sweep(table, tiles, source, share, [(share, bf16), (share, f32)])
        near = [first(n) for n in near]
        (own,) = sweep(table, tiles, source, 3 * share, [(share, f32)])
        last = [second((k + f.astype(f32)).astype(bf16)) for k, f in zip(kept, far)]
        return list(zip(own, near, last))

    once = [(o + n.astype(f32) + t.astype(f32)).astype(bf16) for o, n, t in couple(whole)]
    parts = [couple(panel_of(o, n_row))[0] for o in once]
    twice = []
    for i, part in enumerate(parts):
        twice = [finish(*part, i * CHUNK, source_columns.shape, twice)]
    return twice[0]


def solution(mesh):
    n_row, n_col = mesh.shape["row"], mesh.shape["col"]
    assert n_col == 4
    placed = (
        P(("mem", "row", "col"), None),
        P(("mem", "row"), "col", None, None, None),
        P(("mem", "row"), "col", None, None),
        P(("mem", "row"), "col"),
    )
    return jax.shard_map(
        functools.partial(local, n_row, n_col),
        mesh=mesh,
        in_specs=placed,
        out_specs=P(("mem", "row", "col"), None),
        check_vma=False,
    )
```

```python
import functools

import jax
import jax.numpy as jnp
from jax import lax
from jax.experimental import pallas as pl
from jax.experimental.pallas import tpu as pltpu
from jax.sharding import PartitionSpec as P

TILE_SIZE = 128
BLOCK_ROWS = 32
COL_SHIFT = 16
CHUNK = 128
LOADS = 4

VMEM = pl.BlockSpec(memory_space=pltpu.VMEM)
SMEM = pl.BlockSpec(memory_space=pltpu.SMEM)
HBM = pl.BlockSpec(memory_space=pltpu.HBM)


def directions():
    core = lax.axis_index("row") % 2
    return 1 + core, 2 - core


def load_kernel(own_first, share, blocks, index, count, tiles, table, tiles_here, index_here, count_here, rows, sem):
    slots = tiles.shape[0]
    part = slots // LOADS
    small = [
        pltpu.make_async_copy(index, index_here.at[0:2], sem.at[LOADS]),
        pltpu.make_async_copy(count, count_here, sem.at[LOADS + 1]),
    ]
    copies = [
        pltpu.make_async_copy(
            tiles.at[pl.ds(i * part, part)], tiles_here.at[pl.ds(i * part, part)], sem.at[i]
        )
        for i in range(LOADS)
    ]
    for copy in small + copies:
        copy.start()
    lane = lax.broadcasted_iota(jnp.int32, (BLOCK_ROWS, TILE_SIZE), 1)
    quarter = lane // share
    first, second = directions()
    flip = jnp.where(quarter == 0, 3, jnp.where(quarter == 1, first, jnp.where(quarter == 2, second, 0)))
    wanted = (lax.axis_index("col") ^ flip) * share + lane % share
    slot = lax.broadcasted_iota(jnp.int32, (BLOCK_ROWS, 1), 0)
    for copy in small:
        copy.wait()
    by_slot = index_here[...].T
    for level in range(slots // BLOCK_ROWS):
        here = by_slot[level * BLOCK_ROWS : (level + 1) * BLOCK_ROWS]
        row, block = here[:, 0:1], here[:, 1:2]
        if own_first:
            block = block ^ (lax.axis_index("row") * share)
        block = jnp.where(level * BLOCK_ROWS < count_here[0, 0], block, blocks)
        entry = ((slot + level * BLOCK_ROWS) << COL_SHIFT) | block
        rows[level : level + 1] = jnp.sum(jnp.where(row == wanted, entry, 0), axis=0, keepdims=True)
    to_scalar = pltpu.make_async_copy(rows, table, sem.at[LOADS])
    to_scalar.start()
    to_scalar.wait()
    for copy in copies:
        copy.wait()


def load(tile_index, tile_count, tiles, own_first, share, blocks):
    slots = tiles.shape[0]
    levels = slots // BLOCK_ROWS
    return pl.pallas_call(
        functools.partial(load_kernel, own_first, share, blocks),
        out_shape=[pltpu.SMEM((levels, TILE_SIZE), jnp.int32), pltpu.VMEM(tiles.shape, tiles.dtype)],
        in_specs=[HBM, HBM, HBM],
        out_specs=[SMEM, VMEM],
        scratch_shapes=[
            pltpu.VMEM((8, slots), jnp.int32),
            pltpu.SMEM((1, 1), jnp.int32),
            pltpu.VMEM((levels, TILE_SIZE), jnp.int32),
            pltpu.SemaphoreType.DMA((LOADS + 2,)),
        ],
        compiler_params=pltpu.CompilerParams(vmem_limit_bytes=50 << 20),
    )(tile_index, tile_count, tiles)


def sweep_kernel(counts, first, sources, *refs):
    table, tiles = refs[:2]
    source_refs = refs[2 : 2 + sources]
    out_refs = refs[2 + sources : -1]
    panel = refs[-1]
    at = 0
    for source in source_refs:
        panel[at : at + source.shape[0]] = source[...]
        at += source.shape[0]
    panel[at] = jnp.zeros_like(panel[at])
    levels = table.shape[0]
    split = panel.shape[2] // CHUNK
    for i, count in enumerate(counts):
        outs = out_refs[i * split : (i + 1) * split]

        def row(b, carry, outs=outs, first=first):
            left, right = [], []
            for k in range(levels):
                entry = table[k, first + b]
                left.append(tiles[entry >> COL_SHIFT])
                right.append(panel[entry & ((1 << COL_SHIFT) - 1)])
            total = jnp.dot(
                jnp.concatenate(left, 1), jnp.concatenate(right, 0), preferred_element_type=jnp.float32
            )
            for j, out in enumerate(outs):
                out[b] = total[:, j * CHUNK : (j + 1) * CHUNK].astype(out.dtype)
            return carry

        lax.fori_loop(0, count, row, 0, unroll=8)
        first += count


def sweep(table, tiles, sources, first, outs):
    blocks = sum(s.shape[0] for s in sources)
    columns = sources[0].shape[2]
    split = columns // CHUNK
    out = pl.pallas_call(
        functools.partial(sweep_kernel, [n for n, _ in outs], first, len(sources)),
        out_shape=[
            jax.ShapeDtypeStruct((n, TILE_SIZE, CHUNK), dtype) for n, dtype in outs for _ in range(split)
        ],
        in_specs=[SMEM] + [VMEM] * (1 + len(sources)),
        out_specs=[VMEM] * (len(outs) * split),
        scratch_shapes=[pltpu.VMEM((blocks + 1, TILE_SIZE, columns), jnp.bfloat16)],
        compiler_params=pltpu.CompilerParams(vmem_limit_bytes=12 << 20),
    )(table, tiles, *sources)
    return [out[i * split : (i + 1) * split] for i in range(len(outs))]


def finish_kernel(column, own, near, last, *refs):
    out, here, sem = refs[-3:]
    count = own.shape[0]
    copies = []
    for b in range(count):
        total = own[b] + near[b].astype(jnp.float32) + last[b].astype(jnp.float32)
        rows = slice(b * TILE_SIZE, (b + 1) * TILE_SIZE)
        here[rows] = total.astype(here.dtype)
        copies.append(
            pltpu.make_async_copy(here.at[rows], out.at[rows, column : column + CHUNK], sem.at[b])
        )
        copies[-1].start()
    for copy in copies:
        copy.wait()


def finish(own, near, last, column, shape, earlier):
    return pl.pallas_call(
        functools.partial(finish_kernel, column),
        out_shape=pltpu.HBM(shape, jnp.bfloat16),
        in_specs=[VMEM] * 3 + [HBM] * len(earlier),
        out_specs=HBM,
        input_output_aliases={3: 0} if earlier else {},
        scratch_shapes=[
            pltpu.VMEM((shape[0], CHUNK), jnp.bfloat16),
            pltpu.SemaphoreType.DMA((own.shape[0],)),
        ],
        compiler_params=pltpu.CompilerParams(vmem_limit_bytes=8 << 20),
    )(own, near, last, *earlier)


def exchange(values, second, n_row, n_col):
    pairs = []
    for r in range(n_row):
        flip = 1 + r % 2
        if second:
            flip = 3 - flip
        pairs += [(r * n_col + c, r * n_col + (c ^ flip)) for c in range(n_col)]
    return lax.ppermute(values, ("row", "col"), pairs)


def panel_of(blocks, n_row):
    if n_row == 2:
        return [blocks, lax.ppermute(blocks, "row", [(0, 1), (1, 0)])]
    return [lax.all_gather(blocks, "row", axis=0, tiled=True)]


def local(n_row, n_col, source_columns, tiles, tile_index, tile_count):
    f32, bf16 = jnp.float32, jnp.bfloat16
    share = BLOCK_ROWS // n_col
    columns = source_columns.shape[1]
    split = columns // CHUNK
    blocks = n_row * share
    whole = panel_of(source_columns.reshape(share, TILE_SIZE, columns), n_row)
    table, tiles = load(
        tile_index.reshape(-1, 2).T, tile_count, tiles.reshape(-1, TILE_SIZE, TILE_SIZE), n_row == 2, share, blocks
    )

    first = functools.partial(exchange, second=False, n_row=n_row, n_col=n_col)
    second = functools.partial(exchange, second=True, n_row=n_row, n_col=n_col)

    def couple(source):
        (far,) = sweep(table, tiles, source, 0, [(share, bf16)])
        far = [first(f) for f in far]
        (near,) = sweep(table, tiles, source, share, [(share, bf16)])
        near = [first(n) for n in near]
        kept, own = sweep(table, tiles, source, 2 * share, [(share, f32), (share, f32)])
        last = [second((k + f.astype(f32)).astype(bf16)) for k, f in zip(kept, far)]
        return list(zip(own, near, last))

    once = [(o + n.astype(f32) + t.astype(f32)).astype(bf16) for o, n, t in couple(whole)]
    parts = [couple(panel_of(o, n_row))[0] for o in once]
    twice = []
    for i, part in enumerate(parts):
        twice = [finish(*part, i * CHUNK, source_columns.shape, twice)]
    return twice[0]


def solution(mesh):
    n_row, n_col = mesh.shape["row"], mesh.shape["col"]
    assert n_col == 4
    placed = (
        P(("mem", "row", "col"), None),
        P(("mem", "row"), "col", None, None, None),
        P(("mem", "row"), "col", None, None),
        P(("mem", "row"), "col"),
    )
    return jax.shard_map(
        functools.partial(local, n_row, n_col),
        mesh=mesh,
        in_specs=placed,
        out_specs=P(("mem", "row", "col"), None),
        check_vma=False,
    )
```
